32 devices in a mesh: facet: 8 (over y, x, core), slab: 4 (over z).
Axes of the slice: x: 2, y: 2, z: 4, core: 2. Of those that a mesh axis runs over, the one named last changes fastest.
Arguments:
- slab: bfloat16 [2, 8, 4096, 256], P(None, 'facet', 'slab'), may hold values from -6 to 6
- facet_offset: int32 [8], P('facet'), may hold values from 0 to 28672
- subgrid_offset: int32 [8], replicated, may hold values from 0 to 28672
- vis_cell: int32 [4, 8, 32768], P('slab', 'facet'), may hold values from 0 to 16383
- vis_value: float32 [2, 4, 8, 32768], P(None, 'slab', 'facet'), may hold values from -6 to 6
- vis_weight: float32 [4, 8, 32768], P('slab', 'facet'), may hold values from 0.1 to 1
Outputs:
- residual: float32 [2, 4, 512, 256], P(None, 'slab', 'facet')
- facet_update: float32 [2, 8, 4096, 256], P(None, 'facet', 'slab')
The draws below stay inside these ranges and needn't reach their ends.
All inputs are finite; a program needn't handle non-finite values.
Results may differ from the reference program's by a relative error of at most 0.0041.
Values may be sent and summed in bfloat16 or wider, within the bound.
A program may use at most 64 MiB of HBM per device.

```python
import math
import jax
import jax.numpy as jnp
from jax import lax

IMAGE = 32768
FY = 4096
XW = 256
SG = 256
UVSTEP = 16
SUBGRIDS = 8
FACETS = 8
SLABS = 4
SGR = 64
OWN = 64
VIS_DEV = 32768
N_FACET = 8
N_SLAB = 4


def touch_ends(drawn, stream_key, smallest, high):
    place = [jax.random.randint(jax.random.fold_in(stream_key, axis), (), 0, length) for axis, length in enumerate(drawn.shape)]
    longest = drawn.shape.index(max(drawn.shape))
    neighbour = place[:longest] + [(place[longest] + 1) % drawn.shape[longest]] + place[longest + 1:]
    return drawn.at[tuple(place)].set(smallest).at[tuple(neighbour)].set(high)


def shard_levels(key, dims, cuts, smallest, high):
    gain, own = 1.0, jax.random.fold_in(key, 6)
    for axis_at, blocks in cuts:
        draws = jnp.exp(jax.random.uniform(jax.random.fold_in(own, axis_at), (blocks,), jnp.float32, smallest / len(cuts), high / len(cuts)))
        gain = gain * jnp.repeat(draws, dims[axis_at] // blocks).reshape([-1 if axis == axis_at else 1 for axis in range(len(dims))])
    return gain


def scatter_about(rng, shape, scale, most, split=(), kind=jnp.bfloat16):
    drawn = scale * jax.random.normal(rng, shape, jnp.float32)
    if split:
        drawn = drawn * shard_levels(rng, shape, split, -0.22, 0.18)
    return jnp.clip(drawn, -most, most).astype(kind)


def setup_inputs(seed: int = 0) -> dict:
    keys = jax.random.split(jax.random.key(seed), 7)
    return {
        "slab": scatter_about(keys[0], (2, FACETS, FY, XW), 1.0, 6.0, ((1, 8), (2, 4))),
        "facet_offset": touch_ends(jax.random.randint(keys[1], (FACETS,), 0, IMAGE - FY + 1), jax.random.fold_in(keys[1], 1), 0, IMAGE - FY).astype(jnp.int32),
        "subgrid_offset": touch_ends(jax.random.randint(keys[2], (SUBGRIDS,), 0, IMAGE - UVSTEP * SG + 1), jax.random.fold_in(keys[2], 1), 0, IMAGE - UVSTEP * SG).astype(jnp.int32),
        "vis_cell": touch_ends(jax.random.randint(keys[3], (SLABS, FACETS, VIS_DEV), 0, OWN * XW), jax.random.fold_in(keys[3], 1), 0, (OWN * XW) - 1).astype(jnp.int32),
        "vis_value": scatter_about(keys[4], (2, SLABS, FACETS, VIS_DEV), 1.0, 6.0, ((1, 4), (2, 8)), jnp.float32),
        "vis_weight": jnp.clip(jnp.exp(math.log(1.0) - 2.3025851 * jax.random.uniform(keys[5], (SLABS, FACETS, VIS_DEV), jnp.float32) ** shard_levels(keys[5], (SLABS, FACETS, VIS_DEV), ((0, 4), (1, 8)), -0.2, 0.2)), 0.1, 1.0),
    }


def phase_tables(first_row, local_rows, subgrid_offset):
    freq = subgrid_offset[:, None] + UVSTEP * jnp.arange(SG, dtype=jnp.int32)[None, :]
    places = first_row + jnp.arange(local_rows, dtype=jnp.int32)
    turns = (freq % IMAGE)[:, :, None] * (places % IMAGE)[None, None, :] % IMAGE
    angle = turns.astype(jnp.float32) * (2.0 * math.pi / IMAGE)
    return (jnp.cos(angle).astype(jnp.bfloat16), (-jnp.sin(angle)).astype(jnp.bfloat16))

def reference(slab, facet_offset, subgrid_offset, vis_cell, vis_value, vis_weight):
    scale_fwd = 1.0 / math.sqrt(FY * FACETS)
    scale_back = 1.0 / math.sqrt(SUBGRIDS * SG)

    def forward_step(total, inputs):
        offset, piece = inputs
        tab_real, tab_imag = phase_tables(offset, FY, subgrid_offset)
        tab_real = tab_real.astype(jnp.float32)
        tab_imag = tab_imag.astype(jnp.float32)
        part_real = piece[0].astype(jnp.float32)
        part_imag = piece[1].astype(jnp.float32)
        real = jnp.einsum('skl,lx->skx', tab_real, part_real) - jnp.einsum('skl,lx->skx', tab_imag, part_imag)
        imag = jnp.einsum('skl,lx->skx', tab_real, part_imag) + jnp.einsum('skl,lx->skx', tab_imag, part_real)
        return (total + jnp.stack([real, imag]), None)
    start = jnp.zeros((2, SUBGRIDS, SG, XW), jnp.float32)
    model, _ = lax.scan(forward_step, start, (facet_offset, jnp.moveaxis(slab, 1, 0)))
    model = model * scale_fwd
    model_flat = model.reshape(2, SUBGRIDS, N_SLAB, SGR, XW).transpose(0, 2, 1, 3, 4).reshape(2, -1)
    cells_block = OWN * XW
    base = (jnp.arange(N_SLAB, dtype=jnp.int32)[:, None] * N_FACET + jnp.arange(N_FACET, dtype=jnp.int32)[None, :]) * cells_block
    index = (base[:, :, None] + vis_cell).reshape(-1)
    weighted = (vis_weight[None] * vis_value).reshape(2, -1)
    gridded = jnp.zeros((2, N_SLAB * N_FACET * cells_block), jnp.float32).at[:, index].add(weighted)
    weight_sum = jnp.zeros((N_SLAB * N_FACET * cells_block,), jnp.float32).at[index].add(vis_weight.reshape(-1))
    residual = (gridded - weight_sum[None, :] * model_flat).reshape(2, N_SLAB, SUBGRIDS * SGR, XW)
    sent = residual.astype(jnp.bfloat16)
    whole = sent.reshape(2, N_SLAB, SUBGRIDS, SGR, XW).transpose(0, 2, 1, 3, 4).reshape(2, SUBGRIDS, SG, XW)
    whole = whole.astype(jnp.float32)

    def adjoint_step(offset):
        tab_real, tab_imag = phase_tables(offset, FY, subgrid_offset)
        tab_real = tab_real.astype(jnp.float32)
        tab_imag = tab_imag.astype(jnp.float32)
        real = jnp.einsum('skl,skx->lx', tab_real, whole[0]) + jnp.einsum('skl,skx->lx', tab_imag, whole[1])
        imag = jnp.einsum('skl,skx->lx', tab_real, whole[1]) - jnp.einsum('skl,skx->lx', tab_imag, whole[0])
        return jnp.stack([real, imag]) * scale_back
    updates = lax.map(adjoint_step, facet_offset)
    facet_update = jnp.moveaxis(updates, 0, 1)
    return (residual, facet_update)
```

```python
import functools
import math

import jax
import jax.numpy as jnp
from jax import lax
from jax.experimental import pallas as pl
from jax.experimental.pallas import tpu as pltpu
from jax.sharding import PartitionSpec as P

IMAGE = 32768
SG = 256
UVSTEP = 16
F32 = jnp.float32
BF16 = jnp.bfloat16


def cis(turns):
    turns = turns & (IMAGE - 1)
    quarter = IMAGE // 4
    quad = (turns + quarter // 2) // quarter if quarter & (quarter - 1) else lax.shift_right_logical(
        turns + quarter // 2, quarter.bit_length() - 1
    )
    t = (turns - quad * quarter).astype(F32) * (2.0 * math.pi / IMAGE)
    z = t * t
    s = ((-1.9515295891e-4 * z + 8.3321608736e-3) * z - 1.6666654611e-1) * z * t + t
    c = ((2.443315711809948e-5 * z - 1.388731625493765e-3) * z + 4.166664568298827e-2) * z * z - 0.5 * z + 1.0
    odd = (quad & 1) == 1
    cos = jnp.where(odd, s, c)
    sin = jnp.where(odd, c, s)
    cos = jnp.where(((quad + 1) & 2) == 2, -cos, cos)
    sin = jnp.where((quad & 2) == 2, -sin, sin)
    return cos, sin


def grid_kernel(width, rows, cell_ref, value_ref, weight_ref, out_ref):
    @pl.when(pl.program_id(0) == 0)
    def _():
        out_ref[...] = jnp.zeros_like(out_ref)

    cell = cell_ref[...]
    weight = weight_ref[...]
    chunk = cell.shape[1]
    row = lax.shift_right_logical(cell, width.bit_length() - 1)
    col = cell & (width - 1)
    hot = jnp.where(lax.broadcasted_iota(jnp.int32, (width, chunk), 0) == col, 1.0, 0.0).astype(BF16)
    mine = lax.broadcasted_iota(jnp.int32, (rows, chunk), 0) == row
    terms = [weight * value_ref[0:1, :], weight * value_ref[1:2, :], weight]
    left = jnp.concatenate([jnp.where(mine, t, 0.0).astype(BF16) for t in terms], axis=0)
    out_ref[...] += lax.dot_general(left, hot, (((1,), (1,)), ((), ())), preferred_element_type=F32)


def grid_visibilities(cells, values, weights, owned, width):
    count = cells.shape[1]
    rows = -(-owned // 16) * 16
    chunk = min(count, 2048)
    out = pl.pallas_call(
        functools.partial(grid_kernel, width, rows),
        grid=(count // chunk,),
        in_specs=[
            pl.BlockSpec((1, chunk), lambda i: (0, i)),
            pl.BlockSpec((2, chunk), lambda i: (0, i)),
            pl.BlockSpec((1, chunk), lambda i: (0, i)),
        ],
        out_specs=pl.BlockSpec((3 * rows, width), lambda i: (0, 0)),
        out_shape=jax.ShapeDtypeStruct((3 * rows, width), F32),
        cost_estimate=pl.CostEstimate(flops=6 * rows * width * count, bytes_accessed=16 * count, transcendentals=0),
        name="gridding",
    )(cells, values, weights)
    return out.reshape(3, rows, width)[:, :owned]


def forward_kernel(first_ref, subs_ref, slab_ref, out_ref, cos_ref, sin_ref):
    s = pl.program_id(0)
    rows, local = cos_ref.shape
    first = first_ref[0]

    @pl.when(s == 0)
    def _():
        k = lax.broadcasted_iota(jnp.int32, (rows, local), 0)
        y = lax.broadcasted_iota(jnp.int32, (rows, local), 1) + first
        c, n = cis((UVSTEP * k) * y)
        cos_ref[...] = c
        sin_ref[...] = n

    y = lax.broadcasted_iota(jnp.int32, (8, local), 1) + first
    c1, s1 = cis(subs_ref[s] * y)
    c1, s1 = c1[0:1], s1[0:1]
    c2, s2 = cos_ref[...], sin_ref[...]
    tab_real = (c1 * c2 - s1 * s2).astype(BF16)
    tab_imag = (-(s1 * c2 + c1 * s2)).astype(BF16)
    re, im = slab_ref[0], slab_ref[1]
    dot = functools.partial(jnp.dot, preferred_element_type=F32)
    real = dot(tab_real, re) - dot(tab_imag, im)
    imag = dot(tab_real, im) + dot(tab_imag, re)
    slabs, band = out_ref.shape[1], out_ref.shape[3]
    for p in range(slabs):
        out_ref[0, p, 0] = real[p * band:(p + 1) * band].astype(out_ref.dtype)
        out_ref[1, p, 0] = imag[p * band:(p + 1) * band].astype(out_ref.dtype)


def forward(first, subs, slab, slabs):
    _, local, width = slab.shape
    count = subs.shape[0]
    band = SG // slabs
    return pl.pallas_call(
        forward_kernel,
        grid=(count,),
        in_specs=[
            pl.BlockSpec(memory_space=pltpu.SMEM),
            pl.BlockSpec(memory_space=pltpu.SMEM),
            pl.BlockSpec((2, local, width), lambda s: (0, 0, 0)),
        ],
        out_specs=pl.BlockSpec((2, slabs, 1, band, width), lambda s: (0, 0, s, 0, 0)),
        out_shape=jax.ShapeDtypeStruct((2, slabs, count, band, width), BF16),
        scratch_shapes=[pltpu.VMEM((SG, local), F32), pltpu.VMEM((SG, local), F32)],
        name="forward",
    )(first, subs, slab)


def adjoint_kernel(scale, slabs, first_ref, subs_ref, sent_ref, out_ref):
    tile = out_ref.shape[1]
    count = subs_ref.shape[1]
    band = SG // slabs
    start = first_ref[0] + pl.program_id(0) * tile
    yk = lax.broadcasted_iota(jnp.int32, (tile, SG), 0) + start
    c2, s2 = cis((UVSTEP * lax.broadcasted_iota(jnp.int32, (tile, SG), 1)) * yk)
    ys = lax.broadcasted_iota(jnp.int32, (tile, count), 0) + start
    c1, s1 = cis(ys * subs_ref[...])
    real = jnp.zeros(out_ref.shape[1:], F32)
    imag = jnp.zeros(out_ref.shape[1:], F32)
    dot = functools.partial(jnp.dot, preferred_element_type=F32)
    for s in range(count):
        a, b = c1[:, s:s + 1], s1[:, s:s + 1]
        tab_real = (a * c2 - b * s2).astype(BF16)
        tab_imag = (-(b * c2 + a * s2)).astype(BF16)
        re = jnp.concatenate([sent_ref[0, p, s] for p in range(slabs)], axis=0)
        im = jnp.concatenate([sent_ref[1, p, s] for p in range(slabs)], axis=0)
        real += dot(tab_real, re) + dot(tab_imag, im)
        imag += dot(tab_real, im) - dot(tab_imag, re)
    out_ref[0] = real * scale
    out_ref[1] = imag * scale


def adjoint(first, subs, sent, local):
    _, slabs, count, band, width = sent.shape
    tile = min(local, 256)
    return pl.pallas_call(
        functools.partial(adjoint_kernel, 1.0 / math.sqrt(count * SG), slabs),
        grid=(local // tile,),
        in_specs=[
            pl.BlockSpec(memory_space=pltpu.SMEM),
            pl.BlockSpec((1, count), lambda i: (0, 0)),
            pl.BlockSpec((2, slabs, count, band, width), lambda i: (0, 0, 0, 0, 0)),
        ],
        out_specs=pl.BlockSpec((2, tile, width), lambda i: (0, i, 0)),
        out_shape=jax.ShapeDtypeStruct((2, local, width), F32),
        name="adjoint",
    )(first, subs[None, :], sent)


def body(slab, facet_offset, subgrid_offset, vis_cell, vis_value, vis_weight):
    slabs = lax.axis_size("slab")
    facets = lax.axis_size("facet")
    local_rows = slab.shape[2]
    width = slab.shape[3]
    count_sub = subgrid_offset.shape[0]
    band = SG // slabs
    owned = count_sub * band // facets
    first = (facet_offset + lax.axis_index("slab") * local_rows).astype(jnp.int32)
    sums = grid_visibilities(vis_cell[0], vis_value[:, 0, 0], vis_weight[0], owned, width)
    contrib = forward(first, subgrid_offset, slab[:, 0], slabs)
    contrib = contrib.reshape(2, slabs, facets, owned, width)
    parts = lax.all_to_all(contrib, "facet", 2, 2, tiled=True)
    parts = jnp.sum(parts, axis=2, dtype=F32).astype(BF16)
    parts = lax.all_to_all(parts, "slab", 1, 1, tiled=True)
    scale = 1.0 / math.sqrt(local_rows * slabs * facets)
    model = jnp.sum(parts, axis=1, dtype=F32) * scale
    residual = sums[:2] - sums[2:] * model
    sent = residual.astype(BF16).reshape(2, 1, 1, owned, width)
    piece = lax.all_gather(sent, "slab", axis=1, tiled=True)
    piece = lax.all_gather(piece, "facet", axis=2, tiled=True)
    piece = piece.reshape(2, slabs, count_sub, band, width)
    update = adjoint(first, subgrid_offset, piece, local_rows)
    return (residual.reshape(2, 1, owned, width), update.reshape(2, 1, local_rows, width))


def solution(mesh):
    placed = (
        P(None, "facet", "slab", None),
        P("facet"),
        P(),
        P("slab", "facet", None),
        P(None, "slab", "facet", None),
        P("slab", "facet", None),
    )
    return jax.shard_map(
        body,
        mesh=mesh,
        in_specs=placed,
        out_specs=(P(None, "slab", "facet", None), P(None, "facet", "slab", None)),
        check_vma=False,
    )
```

```python
import functools
import math

import jax
import jax.numpy as jnp
from jax import lax
from jax.experimental import pallas as pl
from jax.experimental.pallas import tpu as pltpu
from jax.sharding import PartitionSpec as P

IMAGE = 32768
SG = 256
UVSTEP = 16
F32 = jnp.float32
BF16 = jnp.bfloat16


def cis(turns):
    turns = turns & (IMAGE - 1)
    quarter = IMAGE // 4
    quad = (turns + quarter // 2) // quarter if quarter & (quarter - 1) else lax.shift_right_logical(
        turns + quarter // 2, quarter.bit_length() - 1
    )
    t = (turns - quad * quarter).astype(F32) * (2.0 * math.pi / IMAGE)
    z = t * t
    s = ((-1.9515295891e-4 * z + 8.3321608736e-3) * z - 1.6666654611e-1) * z * t + t
    c = ((2.443315711809948e-5 * z - 1.388731625493765e-3) * z + 4.166664568298827e-2) * z * z - 0.5 * z + 1.0
    odd = (quad & 1) == 1
    cos = jnp.where(odd, s, c)
    sin = jnp.where(odd, c, s)
    cos = jnp.where(((quad + 1) & 2) == 2, -cos, cos)
    sin = jnp.where((quad & 2) == 2, -sin, sin)
    return cos, sin


def grid_kernel(width, rows, cell_ref, value_ref, weight_ref, out_ref):
    @pl.when(pl.program_id(0) == 0)
    def _():
        out_ref[...] = jnp.zeros_like(out_ref)

    cell = cell_ref[...]
    weight = weight_ref[...]
    chunk = cell.shape[1]
    row = lax.shift_right_logical(cell, width.bit_length() - 1)
    col = cell & (width - 1)
    hot = jnp.where(lax.broadcasted_iota(jnp.int32, (width, chunk), 0) == col, 1.0, 0.0).astype(BF16)
    mine = lax.broadcasted_iota(jnp.int32, (rows, chunk), 0) == row
    terms = [weight * value_ref[0:1, :], weight * value_ref[1:2, :], weight]
    left = jnp.concatenate([jnp.where(mine, t, 0.0).astype(BF16) for t in terms], axis=0)
    out_ref[...] += lax.dot_general(left, hot, (((1,), (1,)), ((), ())), preferred_element_type=F32)


def grid_visibilities(cells, values, weights, owned, width):
    count = cells.shape[1]
    rows = -(-owned // 16) * 16
    chunk = min(count, 2048)
    out = pl.pallas_call(
        functools.partial(grid_kernel, width, rows),
        grid=(count // chunk,),
        in_specs=[
            pl.BlockSpec((1, chunk), lambda i: (0, i)),
            pl.BlockSpec((2, chunk), lambda i: (0, i)),
            pl.BlockSpec((1, chunk), lambda i: (0, i)),
        ],
        out_specs=pl.BlockSpec((3 * rows, width), lambda i: (0, 0)),
        out_shape=jax.ShapeDtypeStruct((3 * rows, width), F32),
        cost_estimate=pl.CostEstimate(flops=6 * rows * width * count, bytes_accessed=16 * count, transcendentals=0),
        name="gridding",
    )(cells, values, weights)
    return out.reshape(3, rows, width)[:, :owned]


def forward_kernel(first_ref, subs_ref, slab_ref, out_ref, cos_ref, sin_ref):
    s = pl.program_id(0)
    rows, local = cos_ref.shape
    first = first_ref[0]

    @pl.when(s == 0)
    def _():
        k = lax.broadcasted_iota(jnp.int32, (rows, local), 0)
        y = lax.broadcasted_iota(jnp.int32, (rows, local), 1) + first
        c, n = cis((UVSTEP * k) * y)
        cos_ref[...] = c
        sin_ref[...] = n

    y = lax.broadcasted_iota(jnp.int32, (8, local), 1) + first
    c1, s1 = cis(subs_ref[s] * y)
    c1, s1 = c1[0:1], s1[0:1]
    c2, s2 = cos_ref[...], sin_ref[...]
    tab_real = (c1 * c2 - s1 * s2).astype(BF16)
    tab_imag = (-(s1 * c2 + c1 * s2)).astype(BF16)
    re, im = slab_ref[0], slab_ref[1]
    dot = functools.partial(jnp.dot, preferred_element_type=F32)
    real = dot(tab_real, re) - dot(tab_imag, im)
    imag = dot(tab_real, im) + dot(tab_imag, re)
    slabs, band = out_ref.shape[1], out_ref.shape[3]
    for p in range(slabs):
        out_ref[0, p, 0] = real[p * band:(p + 1) * band].astype(out_ref.dtype)
        out_ref[1, p, 0] = imag[p * band:(p + 1) * band].astype(out_ref.dtype)


def forward(first, subs, slab, slabs):
    _, local, width = slab.shape
    count = subs.shape[0]
    band = SG // slabs
    return pl.pallas_call(
        forward_kernel,
        grid=(count,),
        in_specs=[
            pl.BlockSpec(memory_space=pltpu.SMEM),
            pl.BlockSpec(memory_space=pltpu.SMEM),
            pl.BlockSpec((2, local, width), lambda s: (0, 0, 0)),
        ],
        out_specs=pl.BlockSpec((2, slabs, 1, band, width), lambda s: (0, 0, s, 0, 0)),
        out_shape=jax.ShapeDtypeStruct((2, slabs, count, band, width), BF16),
        scratch_shapes=[pltpu.VMEM((SG, local), F32), pltpu.VMEM((SG, local), F32)],
        name="forward",
    )(first, subs, slab)


def adjoint_kernel(scale, slabs, first_ref, subs_ref, sent_ref, out_ref):
    tile = out_ref.shape[1]
    count = subs_ref.shape[1]
    band = SG // slabs
    start = first_ref[0] + pl.program_id(0) * tile
    yk = lax.broadcasted_iota(jnp.int32, (tile, SG), 0) + start
    c2, s2 = cis((UVSTEP * lax.broadcasted_iota(jnp.int32, (tile, SG), 1)) * yk)
    ys = lax.broadcasted_iota(jnp.int32, (tile, count), 0) + start
    c1, s1 = cis(ys * subs_ref[...])
    real = jnp.zeros(out_ref.shape[1:], F32)
    imag = jnp.zeros(out_ref.shape[1:], F32)
    dot = functools.partial(jnp.dot, preferred_element_type=F32)
    for s in range(count):
        a, b = c1[:, s:s + 1], s1[:, s:s + 1]
        tab_real = (a * c2 - b * s2).astype(BF16)
        tab_imag = (-(b * c2 + a * s2)).astype(BF16)
        re = jnp.concatenate([sent_ref[0, p, s] for p in range(slabs)], axis=0)
        im = jnp.concatenate([sent_ref[1, p, s] for p in range(slabs)], axis=0)
        real += dot(tab_real, re) + dot(tab_imag, im)
        imag += dot(tab_real, im) - dot(tab_imag, re)
    out_ref[0] = real * scale
    out_ref[1] = imag * scale


def adjoint(first, subs, sent, local):
    _, slabs, count, band, width = sent.shape
    tile = min(local, 256)
    return pl.pallas_call(
        functools.partial(adjoint_kernel, 1.0 / math.sqrt(count * SG), slabs),
        grid=(local // tile,),
        in_specs=[
            pl.BlockSpec(memory_space=pltpu.SMEM),
            pl.BlockSpec((1, count), lambda i: (0, 0)),
            pl.BlockSpec((2, slabs, count, band, width), lambda i: (0, 0, 0, 0, 0)),
        ],
        out_specs=pl.BlockSpec((2, tile, width), lambda i: (0, i, 0)),
        out_shape=jax.ShapeDtypeStruct((2, local, width), F32),
        name="adjoint",
    )(first, subs[None, :], sent)


def fused_kernel(
    scale, back, subs_ref, subv_ref, places_ref, ycol_ref, slab_ref, cell_ref, value_ref, weight_ref,
    residual_ref, update_ref,
    pslab, pplaces, cos_ref, sin_ref, acc, cb, rx, zf, zb, rz, sums, full, table,
    sw_send, sw_recv, x_send, x_recv, z_send, z_recv, gz_send, gz_recv, gx_send, gx_recv, gc_send, gc_recv,
):
    facets, slabs = lax.axis_size("facet"), lax.axis_size("slab")
    q, z = lax.axis_index("facet"), lax.axis_index("slab")
    core, chip = q % 2, q // 2
    chips = facets // 2
    partner = q + 1 - 2 * core
    _, local, width = slab_ref.shape
    band = SG // slabs
    dot = functools.partial(jnp.dot, preferred_element_type=F32)

    def at_chip(d):
        return 2 * ((chip + d) % chips) + core

    def from_chip(d):
        return 2 * ((chip + chips - d) % chips) + core

    def at_slab(e):
        return (z + e) % slabs

    def from_slab(e):
        return (z + slabs - e) % slabs

    def remote(src, dst, send, recv, **where):
        return pltpu.make_async_remote_copy(
            src_ref=src, dst_ref=dst, send_sem=send, recv_sem=recv,
            device_id=where, device_id_type=pl.DeviceIdType.MESH,
        )

    barrier = pltpu.get_barrier_semaphore()
    pl.semaphore_signal(barrier, inc=1, device_id={"facet": partner}, device_id_type=pl.DeviceIdType.MESH)
    for d in range(1, chips):
        pl.semaphore_signal(barrier, inc=1, device_id={"facet": at_chip(d)}, device_id_type=pl.DeviceIdType.MESH)
    for e in range(1, slabs):
        pl.semaphore_signal(barrier, inc=1, device_id={"slab": at_slab(e)}, device_id_type=pl.DeviceIdType.MESH)
    pl.semaphore_wait(barrier, chips + slabs - 1)

    swap_places = remote(places_ref, pplaces, sw_send.at[0], sw_recv.at[0], facet=partner)
    swap_slab = remote(slab_ref, pslab, sw_send.at[1], sw_recv.at[1], facet=partner)
    swap_places.start()
    swap_slab.start()

    def build(y_ref, slot):
        def step(i, carry):
            k = lax.broadcasted_iota(jnp.int32, (32, local), 0) + i * 32
            c, n = cis((UVSTEP * k) * y_ref[0:1, :])
            at = pl.ds(pl.multiple_of(i * 32, 32), 32)
            cos_ref[slot, at] = c
            sin_ref[slot, at] = n
            return carry

        lax.fori_loop(0, SG // 32, step, 0)

    def partial_sum(s, y_ref, slot, data_ref):
        c1, s1 = cis(subs_ref[s] * y_ref[...])
        c1, s1 = c1[0:1], s1[0:1]
        c2, s2 = cos_ref[slot], sin_ref[slot]
        tab_real = (c1 * c2 - s1 * s2).astype(BF16)
        tab_imag = (-(s1 * c2 + c1 * s2)).astype(BF16)
        re, im = data_ref[0], data_ref[1]
        return dot(tab_real, re) - dot(tab_imag, im), dot(tab_real, im) + dot(tab_imag, re)

    build(places_ref, 0)

    def own_part(d, carry):
        real, imag = partial_sum(at_chip(d), places_ref, 0, slab_ref)
        acc[d, 0] = real
        acc[d, 1] = imag
        return carry

    lax.fori_loop(0, chips, own_part, 0)
    swap_places.wait()
    build(pplaces, 1)
    swap_slab.wait()
    x_copies = []
    for d in list(range(1, chips)) + [0]:
        real, imag = partial_sum(at_chip(d), pplaces, 1, pslab)
        if d == 0:
            acc[0, 0] += real
            acc[0, 1] += imag
        else:
            cb[d - 1, 0] = (acc[d, 0] + real).astype(BF16)
            cb[d - 1, 1] = (acc[d, 1] + imag).astype(BF16)
            copy = remote(cb.at[d - 1], rx.at[d - 1], x_send.at[d - 1], x_recv.at[d - 1], facet=at_chip(d))
            copy.start()
            x_copies.append(copy)

    rows = sums.shape[0] // 3
    count = cell_ref.shape[1]
    chunk = min(count, 2048)
    sums[...] = jnp.zeros_like(sums)

    def grid_step(i, carry):
        at = pl.ds(pl.multiple_of(i * chunk, chunk), chunk)
        cell = cell_ref[:, at]
        weight = weight_ref[:, at]
        row = lax.shift_right_logical(cell, width.bit_length() - 1)
        col = cell & (width - 1)
        hot = jnp.where(lax.broadcasted_iota(jnp.int32, (width, chunk), 0) == col, 1.0, 0.0).astype(BF16)
        mine = lax.broadcasted_iota(jnp.int32, (rows, chunk), 0) == row
        terms = [weight * value_ref[0:1, at], weight * value_ref[1:2, at], weight]
        left = jnp.concatenate([jnp.where(mine, t, 0.0).astype(BF16) for t in terms], axis=0)
        sums[...] += lax.dot_general(left, hot, (((1,), (1,)), ((), ())), preferred_element_type=F32)
        return carry

    lax.fori_loop(0, count // chunk, grid_step, 0)

    for copy in x_copies:
        copy.wait()
    for p in range(slabs):
        for c in range(2):
            at = slice(p * band, (p + 1) * band)
            total = acc[0, c, at]
            for d in range(1, chips):
                total += rx[d - 1, c, at].astype(F32)
            zf[p, c] = total
            zb[p, c] = total.astype(BF16)
    z_copies = []
    for e in range(1, slabs):
        copy = remote(zb.at[at_slab(e)], rz.at[e - 1], z_send.at[e - 1], z_recv.at[e - 1], slab=at_slab(e))
        copy.start()
        z_copies.append(copy)

    tile = min(local, 256)

    def table_step(i, carry):
        at = pl.ds(pl.multiple_of(i * tile, tile), tile)
        y = ycol_ref[at, 0:1]
        c2, s2 = cis((UVSTEP * lax.broadcasted_iota(jnp.int32, (tile, SG), 1)) * y)
        c1, s1 = cis(y * subv_ref[...])
        for s in range(facets):
            a, b = c1[:, s:s + 1], s1[:, s:s + 1]
            table[s, 0, at] = (a * c2 - b * s2).astype(BF16)
            table[s, 1, at] = (-(b * c2 + a * s2)).astype(BF16)
        return carry

    lax.fori_loop(0, local // tile, table_step, 0)

    for copy in z_copies:
        copy.wait()
    for c in range(2):
        model = zf[z, c]
        for e in range(1, slabs):
            model += rz[e - 1, c].astype(F32)
        piece = sums[c * rows:c * rows + band] - sums[2 * rows:2 * rows + band] * (model * scale)
        residual_ref[c] = piece
        full[q, z, c] = piece.astype(BF16)

    late = []

    def spread(s, p, e, d):
        ref = full.at[s, p]
        copy = remote(ref, ref, gc_send.at[e, d], gc_recv.at[e, d], facet=partner)
        copy.start()
        late.append(copy)

    def across(p, e):
        ref = full.at[q, p]
        out = []
        for d in range(1, chips):
            copy = remote(ref, ref, gx_send.at[e, d - 1], gx_recv.at[e, d - 1], facet=at_chip(d))
            copy.start()
            out.append(copy)
        return out

    own = full.at[q, z]
    g_copies = []
    for e in range(1, slabs):
        copy = remote(own, own, gz_send.at[e - 1], gz_recv.at[e - 1], slab=at_slab(e))
        copy.start()
        g_copies.append(copy)
    a_copies = [across(z, 0)]
    spread(q, z, 0, 0)
    for e in range(1, slabs):
        g_copies[e - 1].wait_recv()
        a_copies.append(across(from_slab(e), e))
        spread(q, from_slab(e), e, 0)
    for e in range(slabs):
        for d in range(1, chips):
            a_copies[e][d - 1].wait_recv()
            spread(from_chip(d), from_slab(e), e, d)
    for copy in g_copies:
        copy.wait_send()
    for row in a_copies:
        for copy in row:
            copy.wait_send()
    for copy in late:
        copy.wait()

    def update_step(i, carry):
        at = pl.ds(pl.multiple_of(i * tile, tile), tile)
        real = jnp.zeros((tile, width), F32)
        imag = jnp.zeros((tile, width), F32)
        for s in range(facets):
            tab_real, tab_imag = table[s, 0, at], table[s, 1, at]
            re = jnp.concatenate([full[s, p, 0] for p in range(slabs)], axis=0)
            im = jnp.concatenate([full[s, p, 1] for p in range(slabs)], axis=0)
            real += dot(tab_real, re) + dot(tab_imag, im)
            imag += dot(tab_real, im) - dot(tab_imag, re)
        update_ref[0, at] = real * back
        update_ref[1, at] = imag * back
        return carry

    lax.fori_loop(0, local // tile, update_step, 0)


def fused(first, subs, slab, cells, values, weights, slabs, facets):
    _, local, width = slab.shape
    band = SG // slabs
    chips = facets // 2
    rows = -(-band // 16) * 16
    places = first + lax.broadcasted_iota(jnp.int32, (8, local), 1)
    ycol = first + lax.broadcasted_iota(jnp.int32, (local, 8), 0)
    vmem = pl.BlockSpec(memory_space=pltpu.VMEM)
    dma = pltpu.SemaphoreType.DMA
    return pl.pallas_call(
        functools.partial(
            fused_kernel, 1.0 / math.sqrt(local * slabs * facets), 1.0 / math.sqrt(subs.shape[0] * SG)
        ),
        in_specs=[pl.BlockSpec(memory_space=pltpu.SMEM)] + [vmem] * 7,
        out_specs=[vmem, vmem],
        out_shape=[
            jax.ShapeDtypeStruct((2, band, width), F32),
            jax.ShapeDtypeStruct((2, local, width), F32),
        ],
        scratch_shapes=[
            pltpu.VMEM((2, local, width), BF16),
            pltpu.VMEM((8, local), jnp.int32),
            pltpu.VMEM((2, SG, local), F32),
            pltpu.VMEM((2, SG, local), F32),
            pltpu.VMEM((chips, 2, SG, width), F32),
            pltpu.VMEM((chips - 1, 2, SG, width), BF16),
            pltpu.VMEM((chips - 1, 2, SG, width), BF16),
            pltpu.VMEM((slabs, 2, band, width), F32),
            pltpu.VMEM((slabs, 2, band, width), BF16),
            pltpu.VMEM((slabs - 1, 2, band, width), BF16),
            pltpu.VMEM((3 * rows, width), F32),
            pltpu.VMEM((facets, slabs, 2, band, width), BF16),
            pltpu.VMEM((facets, 2, local, SG), BF16),
            dma((2,)), dma((2,)),
            dma((chips - 1,)), dma((chips - 1,)),
            dma((slabs - 1,)), dma((slabs - 1,)),
            dma((slabs - 1,)), dma((slabs - 1,)),
            dma((slabs, chips - 1)), dma((slabs, chips - 1)),
            dma((slabs, chips)), dma((slabs, chips)),
        ],
        compiler_params=pltpu.CompilerParams(collective_id=0, has_side_effects=True, vmem_limit_bytes=60 * 1024 * 1024),
        name="fused",
    )(subs, subs[None, :], places, ycol, slab, cells, values, weights)


def body(slab, facet_offset, subgrid_offset, vis_cell, vis_value, vis_weight):
    slabs = lax.axis_size("slab")
    facets = lax.axis_size("facet")
    local_rows = slab.shape[2]
    width = slab.shape[3]
    count_sub = subgrid_offset.shape[0]
    band = SG // slabs
    owned = count_sub * band // facets
    first = (facet_offset + lax.axis_index("slab") * local_rows).astype(jnp.int32)
    if owned == band and facets % 2 == 0 and facets > 2 and slabs > 1 and band % 16 == 0:
        residual, update = fused(
            first, subgrid_offset, slab[:, 0], vis_cell[0], vis_value[:, 0, 0], vis_weight[0], slabs, facets
        )
        return (residual.reshape(2, 1, owned, width), update.reshape(2, 1, local_rows, width))
    sums = grid_visibilities(vis_cell[0], vis_value[:, 0, 0], vis_weight[0], owned, width)
    contrib = forward(first, subgrid_offset, slab[:, 0], slabs)
    contrib = contrib.reshape(2, slabs, facets, owned, width)
    parts = lax.all_to_all(contrib, "facet", 2, 2, tiled=True)
    parts = jnp.sum(parts, axis=2, dtype=F32).astype(BF16)
    parts = lax.all_to_all(parts, "slab", 1, 1, tiled=True)
    scale = 1.0 / math.sqrt(local_rows * slabs * facets)
    model = jnp.sum(parts, axis=1, dtype=F32) * scale
    residual = sums[:2] - sums[2:] * model
    sent = residual.astype(BF16).reshape(2, 1, 1, owned, width)
    piece = lax.all_gather(sent, "slab", axis=1, tiled=True)
    piece = lax.all_gather(piece, "facet", axis=2, tiled=True)
    piece = piece.reshape(2, slabs, count_sub, band, width)
    update = adjoint(first, subgrid_offset, piece, local_rows)
    return (residual.reshape(2, 1, owned, width), update.reshape(2, 1, local_rows, width))


def solution(mesh):
    placed = (
        P(None, "facet", "slab", None),
        P("facet"),
        P(),
        P("slab", "facet", None),
        P(None, "slab", "facet", None),
        P("slab", "facet", None),
    )
    return jax.shard_map(
        body,
        mesh=mesh,
        in_specs=placed,
        out_specs=(P(None, "slab", "facet", None), P(None, "facet", "slab", None)),
        check_vma=False,
    )
```

```python
import functools
import math

import jax
import jax.numpy as jnp
from jax import lax
from jax.experimental import pallas as pl
from jax.experimental.pallas import tpu as pltpu
from jax.sharding import PartitionSpec as P

IMAGE = 32768
SG = 256
UVSTEP = 16
F32 = jnp.float32
BF16 = jnp.bfloat16


def cis(turns):
    turns = turns & (IMAGE - 1)
    quarter = IMAGE // 4
    quad = (turns + quarter // 2) // quarter if quarter & (quarter - 1) else lax.shift_right_logical(
        turns + quarter // 2, quarter.bit_length() - 1
    )
    t = (turns - quad * quarter).astype(F32) * (2.0 * math.pi / IMAGE)
    z = t * t
    s = ((-1.9515295891e-4 * z + 8.3321608736e-3) * z - 1.6666654611e-1) * z * t + t
    c = ((2.443315711809948e-5 * z - 1.388731625493765e-3) * z + 4.166664568298827e-2) * z * z - 0.5 * z + 1.0
    odd = (quad & 1) == 1
    cos = jnp.where(odd, s, c)
    sin = jnp.where(odd, c, s)
    cos = jnp.where(((quad + 1) & 2) == 2, -cos, cos)
    sin = jnp.where((quad & 2) == 2, -sin, sin)
    return cos, sin


def grid_kernel(width, rows, cell_ref, value_ref, weight_ref, out_ref):
    @pl.when(pl.program_id(0) == 0)
    def _():
        out_ref[...] = jnp.zeros_like(out_ref)

    cell = cell_ref[...]
    weight = weight_ref[...]
    chunk = cell.shape[1]
    row = lax.shift_right_logical(cell, width.bit_length() - 1)
    col = cell & (width - 1)
    hot = jnp.where(lax.broadcasted_iota(jnp.int32, (width, chunk), 0) == col, 1.0, 0.0).astype(BF16)
    mine = lax.broadcasted_iota(jnp.int32, (rows, chunk), 0) == row
    terms = [weight * value_ref[0:1, :], weight * value_ref[1:2, :], weight]
    left = jnp.concatenate([jnp.where(mine, t, 0.0).astype(BF16) for t in terms], axis=0)
    out_ref[...] += lax.dot_general(left, hot, (((1,), (1,)), ((), ())), preferred_element_type=F32)


def grid_visibilities(cells, values, weights, owned, width):
    count = cells.shape[1]
    rows = -(-owned // 16) * 16
    chunk = min(count, 2048)
    out = pl.pallas_call(
        functools.partial(grid_kernel, width, rows),
        grid=(count // chunk,),
        in_specs=[
            pl.BlockSpec((1, chunk), lambda i: (0, i)),
            pl.BlockSpec((2, chunk), lambda i: (0, i)),
            pl.BlockSpec((1, chunk), lambda i: (0, i)),
        ],
        out_specs=pl.BlockSpec((3 * rows, width), lambda i: (0, 0)),
        out_shape=jax.ShapeDtypeStruct((3 * rows, width), F32),
        cost_estimate=pl.CostEstimate(flops=6 * rows * width * count, bytes_accessed=16 * count, transcendentals=0),
        name="gridding",
    )(cells, values, weights)
    return out.reshape(3, rows, width)[:, :owned]


def forward_kernel(first_ref, subs_ref, slab_ref, out_ref, cos_ref, sin_ref):
    s = pl.program_id(0)
    rows, local = cos_ref.shape
    first = first_ref[0]

    @pl.when(s == 0)
    def _():
        k = lax.broadcasted_iota(jnp.int32, (rows, local), 0)
        y = lax.broadcasted_iota(jnp.int32, (rows, local), 1) + first
        c, n = cis((UVSTEP * k) * y)
        cos_ref[...] = c
        sin_ref[...] = n

    y = lax.broadcasted_iota(jnp.int32, (8, local), 1) + first
    c1, s1 = cis(subs_ref[s] * y)
    c1, s1 = c1[0:1], s1[0:1]
    c2, s2 = cos_ref[...], sin_ref[...]
    tab_real = (c1 * c2 - s1 * s2).astype(BF16)
    tab_imag = (-(s1 * c2 + c1 * s2)).astype(BF16)
    re, im = slab_ref[0], slab_ref[1]
    dot = functools.partial(jnp.dot, preferred_element_type=F32)
    real = dot(tab_real, re) - dot(tab_imag, im)
    imag = dot(tab_real, im) + dot(tab_imag, re)
    slabs, band = out_ref.shape[1], out_ref.shape[3]
    for p in range(slabs):
        out_ref[0, p, 0] = real[p * band:(p + 1) * band].astype(out_ref.dtype)
        out_ref[1, p, 0] = imag[p * band:(p + 1) * band].astype(out_ref.dtype)


def forward(first, subs, slab, slabs):
    _, local, width = slab.shape
    count = subs.shape[0]
    band = SG // slabs
    return pl.pallas_call(
        forward_kernel,
        grid=(count,),
        in_specs=[
            pl.BlockSpec(memory_space=pltpu.SMEM),
            pl.BlockSpec(memory_space=pltpu.SMEM),
            pl.BlockSpec((2, local, width), lambda s: (0, 0, 0)),
        ],
        out_specs=pl.BlockSpec((2, slabs, 1, band, width), lambda s: (0, 0, s, 0, 0)),
        out_shape=jax.ShapeDtypeStruct((2, slabs, count, band, width), BF16),
        scratch_shapes=[pltpu.VMEM((SG, local), F32), pltpu.VMEM((SG, local), F32)],
        name="forward",
    )(first, subs, slab)


def adjoint_kernel(scale, slabs, first_ref, subs_ref, sent_ref, out_ref):
    tile = out_ref.shape[1]
    count = subs_ref.shape[1]
    band = SG // slabs
    start = first_ref[0] + pl.program_id(0) * tile
    yk = lax.broadcasted_iota(jnp.int32, (tile, SG), 0) + start
    c2, s2 = cis((UVSTEP * lax.broadcasted_iota(jnp.int32, (tile, SG), 1)) * yk)
    ys = lax.broadcasted_iota(jnp.int32, (tile, count), 0) + start
    c1, s1 = cis(ys * subs_ref[...])
    real = jnp.zeros(out_ref.shape[1:], F32)
    imag = jnp.zeros(out_ref.shape[1:], F32)
    dot = functools.partial(jnp.dot, preferred_element_type=F32)
    for s in range(count):
        a, b = c1[:, s:s + 1], s1[:, s:s + 1]
        tab_real = (a * c2 - b * s2).astype(BF16)
        tab_imag = (-(b * c2 + a * s2)).astype(BF16)
        re = jnp.concatenate([sent_ref[0, p, s] for p in range(slabs)], axis=0)
        im = jnp.concatenate([sent_ref[1, p, s] for p in range(slabs)], axis=0)
        real += dot(tab_real, re) + dot(tab_imag, im)
        imag += dot(tab_real, im) - dot(tab_imag, re)
    out_ref[0] = real * scale
    out_ref[1] = imag * scale


def adjoint(first, subs, sent, local):
    _, slabs, count, band, width = sent.shape
    tile = min(local, 256)
    return pl.pallas_call(
        functools.partial(adjoint_kernel, 1.0 / math.sqrt(count * SG), slabs),
        grid=(local // tile,),
        in_specs=[
            pl.BlockSpec(memory_space=pltpu.SMEM),
            pl.BlockSpec((1, count), lambda i: (0, 0)),
            pl.BlockSpec((2, slabs, count, band, width), lambda i: (0, 0, 0, 0, 0)),
        ],
        out_specs=pl.BlockSpec((2, tile, width), lambda i: (0, i, 0)),
        out_shape=jax.ShapeDtypeStruct((2, local, width), F32),
        name="adjoint",
    )(first, subs[None, :], sent)


def fused_kernel(
    scale, back, subs_ref, offset_ref, subv_ref, offv_ref, slab_ref, cell_ref, value_ref, weight_ref,
    residual_ref, update_ref,
    pslab, poff, cos_ref, sin_ref, acc, cb, rx, zf, zb, rz, sums, full, table,
    sw_send, sw_recv, x_send, x_recv, z_send, z_recv, gz_send, gz_recv, gx_send, gx_recv, gc_send, gc_recv,
):
    facets, slabs = lax.axis_size("facet"), lax.axis_size("slab")
    q, z = lax.axis_index("facet"), lax.axis_index("slab")
    core, chip = q % 2, q // 2
    chips = facets // 2
    partner = q + 1 - 2 * core
    _, local, width = slab_ref.shape
    band = SG // slabs
    dot = functools.partial(jnp.dot, preferred_element_type=F32)

    def at_chip(d):
        return 2 * ((chip + d) % chips) + core

    def from_chip(d):
        return 2 * ((chip + chips - d) % chips) + core

    def at_slab(e):
        return (z + e) % slabs

    def from_slab(e):
        return (z + slabs - e) % slabs

    def remote(src, dst, send, recv, **where):
        return pltpu.make_async_remote_copy(
            src_ref=src, dst_ref=dst, send_sem=send, recv_sem=recv,
            device_id=where, device_id_type=pl.DeviceIdType.MESH,
        )

    barrier = pltpu.get_barrier_semaphore()
    pl.semaphore_signal(barrier, inc=1, device_id={"facet": partner}, device_id_type=pl.DeviceIdType.MESH)
    for d in range(1, chips):
        pl.semaphore_signal(barrier, inc=1, device_id={"facet": at_chip(d)}, device_id_type=pl.DeviceIdType.MESH)
    for e in range(1, slabs):
        pl.semaphore_signal(barrier, inc=1, device_id={"slab": at_slab(e)}, device_id_type=pl.DeviceIdType.MESH)
    pl.semaphore_wait(barrier, chips + slabs - 1)

    swap_offset = remote(offv_ref, poff, sw_send.at[0], sw_recv.at[0], facet=partner)
    swap_slab = remote(slab_ref, pslab, sw_send.at[1], sw_recv.at[1], facet=partner)
    swap_offset.start()
    swap_slab.start()

    first = offset_ref[0] + z * local

    def build(y, slot):
        def step(i, carry):
            k = lax.broadcasted_iota(jnp.int32, (32, local), 0) + i * 32
            c, n = cis((UVSTEP * k) * y[0:1, :])
            at = pl.ds(pl.multiple_of(i * 32, 32), 32)
            cos_ref[slot, at] = c
            sin_ref[slot, at] = n
            return carry

        lax.fori_loop(0, SG // 32, step, 0)

    def partial_sum(s, y, slot, data_ref):
        c1, s1 = cis(subs_ref[s] * y)
        c1, s1 = c1[0:1], s1[0:1]
        c2, s2 = cos_ref[slot], sin_ref[slot]
        tab_real = (c1 * c2 - s1 * s2).astype(BF16)
        tab_imag = (-(s1 * c2 + c1 * s2)).astype(BF16)
        re, im = data_ref[0], data_ref[1]
        return dot(tab_real, re) - dot(tab_imag, im), dot(tab_real, im) + dot(tab_imag, re)

    line = lax.broadcasted_iota(jnp.int32, (8, local), 1)
    places = line + first
    build(places, 0)

    def own_part(d, carry):
        real, imag = partial_sum(at_chip(d), places, 0, slab_ref)
        acc[d, 0] = real
        acc[d, 1] = imag
        return carry

    lax.fori_loop(0, chips, own_part, 0)
    swap_offset.wait()
    pplaces = line + (poff[:, 0:1] + z * local)
    build(pplaces, 1)
    swap_slab.wait()
    x_copies = []
    for d in list(range(1, chips)) + [0]:
        real, imag = partial_sum(at_chip(d), pplaces, 1, pslab)
        if d == 0:
            acc[0, 0] += real
            acc[0, 1] += imag
        else:
            cb[d - 1, 0] = (acc[d, 0] + real).astype(BF16)
            cb[d - 1, 1] = (acc[d, 1] + imag).astype(BF16)
            copy = remote(cb.at[d - 1], rx.at[d - 1], x_send.at[d - 1], x_recv.at[d - 1], facet=at_chip(d))
            copy.start()
            x_copies.append(copy)

    rows = sums.shape[0] // 3
    count = cell_ref.shape[1]
    chunk = min(count, 2048)
    sums[...] = jnp.zeros_like(sums)

    def grid_step(i, carry):
        at = pl.ds(pl.multiple_of(i * chunk, chunk), chunk)
        cell = cell_ref[:, at]
        weight = weight_ref[:, at]
        row = lax.shift_right_logical(cell, width.bit_length() - 1).astype(F32)
        col = (cell & (width - 1)).astype(F32)
        lines = lax.broadcasted_iota(jnp.int32, (16, chunk), 0).astype(F32).astype(BF16)
        row = jnp.broadcast_to(row, (16, chunk)).astype(BF16)
        col = jnp.broadcast_to(col, (16, chunk)).astype(BF16)
        one, zero = jnp.ones((16, chunk), BF16), jnp.zeros((16, chunk), BF16)
        hot = jnp.concatenate(
            [jnp.where(col == lines + jnp.asarray(g, BF16), one, zero) for g in range(0, width, 16)], axis=0
        )
        terms = [weight * value_ref[0, :, at], weight * value_ref[1, :, at], weight]
        terms = [jnp.broadcast_to(t, (16, chunk)).astype(BF16) for t in terms]
        left = jnp.concatenate(
            [jnp.where(row == lines + jnp.asarray(g, BF16), t, zero) for t in terms for g in range(0, rows, 16)],
            axis=0,
        )
        sums[...] += lax.dot_general(left, hot, (((1,), (1,)), ((), ())), preferred_element_type=F32)
        return carry

    chunks = count // chunk
    early = (5 * chunks) // 8
    lax.fori_loop(0, early, grid_step, 0)

    for copy in x_copies:
        copy.wait()
    for p in range(slabs):
        for c in range(2):
            at = slice(p * band, (p + 1) * band)
            total = acc[0, c, at]
            for d in range(1, chips):
                total += rx[d - 1, c, at].astype(F32)
            zf[p, c] = total
            zb[p, c] = total.astype(BF16)
    z_copies = []
    for e in range(1, slabs):
        copy = remote(zb.at[at_slab(e)], rz.at[e - 1], z_send.at[e - 1], z_recv.at[e - 1], slab=at_slab(e))
        copy.start()
        z_copies.append(copy)

    tile = min(local, 256)

    lax.fori_loop(early, chunks, grid_step, 0)

    for copy in z_copies:
        copy.wait()
    for c in range(2):
        model = zf[z, c]
        for e in range(1, slabs):
            model += rz[e - 1, c].astype(F32)
        piece = sums[c * rows:c * rows + band] - sums[2 * rows:2 * rows + band] * (model * scale)
        residual_ref[c] = piece
        full[q, z, c] = piece.astype(BF16)

    def table_step(i, carry):
        at = pl.ds(pl.multiple_of(i * tile, tile), tile)
        y = lax.broadcasted_iota(jnp.int32, (tile, 1), 0) + (first + i * tile)
        c2, s2 = cis((UVSTEP * lax.broadcasted_iota(jnp.int32, (tile, SG), 1)) * y)
        c1, s1 = cis(y * subv_ref[...])
        for s in range(facets):
            a, b = c1[:, s:s + 1], s1[:, s:s + 1]
            table[s, 0, at] = (a * c2 - b * s2).astype(BF16)
            table[s, 1, at] = (-(b * c2 + a * s2)).astype(BF16)
        return carry

    late = []

    def spread(s, p, e, d):
        ref = full.at[s, p]
        copy = remote(ref, ref, gc_send.at[e, d], gc_recv.at[e, d], facet=partner)
        copy.start()
        late.append(copy)

    def across(p, e):
        ref = full.at[q, p]
        out = []
        for d in range(1, chips):
            copy = remote(ref, ref, gx_send.at[e, d - 1], gx_recv.at[e, d - 1], facet=at_chip(d))
            copy.start()
            out.append(copy)
        return out

    own = full.at[q, z]
    g_copies = []
    for e in range(1, slabs):
        copy = remote(own, own, gz_send.at[e - 1], gz_recv.at[e - 1], slab=at_slab(e))
        copy.start()
        g_copies.append(copy)
    a_copies = [across(z, 0)]
    spread(q, z, 0, 0)
    tiles = local // tile
    done = 0
    for e in range(1, slabs):
        share = (e * tiles) // slabs
        lax.fori_loop(done, share, table_step, 0)
        done = share
        g_copies[e - 1].wait_recv()
        a_copies.append(across(from_slab(e), e))
        spread(q, from_slab(e), e, 0)
    lax.fori_loop(done, tiles, table_step, 0)

    def update_pass(which, begin, end):
        def step(i, carry):
            at = pl.ds(pl.multiple_of(i * tile, tile), tile)
            real = imag = None
            for s in which:
                tab_real, tab_imag = table[s, 0, at], table[s, 1, at]
                re = jnp.concatenate([full[s, p, 0] for p in range(slabs)], axis=0)
                im = jnp.concatenate([full[s, p, 1] for p in range(slabs)], axis=0)
                dr = dot(tab_real, re) + dot(tab_imag, im)
                di = dot(tab_real, im) - dot(tab_imag, re)
                real = dr if real is None else real + dr
                imag = di if imag is None else imag + di
            if not begin:
                real += update_ref[0, at]
                imag += update_ref[1, at]
            update_ref[0, at] = real * back if end else real
            update_ref[1, at] = imag * back if end else imag
            return carry

        lax.fori_loop(0, tiles, step, 0)

    def relay(e):
        for d in range(1, chips):
            a_copies[e][d - 1].wait_recv()
            spread(from_chip(d), from_slab(e), e, d)

    relay(0)
    update_pass([q], True, False)
    for e in range(1, slabs - 1):
        relay(e)
    for copy in late[:slabs]:
        copy.wait_recv()
    update_pass([partner], False, False)
    relay(slabs - 1)
    update_pass([from_chip(d) for d in range(1, chips)], False, False)
    for copy in late[slabs:]:
        copy.wait_recv()
    update_pass([from_chip(d) + 1 - 2 * core for d in range(1, chips)], False, True)
    for copy in g_copies + late:
        copy.wait_send()
    for group in a_copies:
        for copy in group:
            copy.wait_send()


def fused(offset, subs, slab, cells, values, weights, slabs, facets):
    _, local, width = slab.shape
    band = SG // slabs
    chips = facets // 2
    rows = -(-band // 16) * 16
    vmem = pl.BlockSpec(memory_space=pltpu.VMEM)
    dma = pltpu.SemaphoreType.DMA
    return pl.pallas_call(
        functools.partial(
            fused_kernel, 1.0 / math.sqrt(local * slabs * facets), 1.0 / math.sqrt(subs.shape[0] * SG)
        ),
        in_specs=[pl.BlockSpec(memory_space=pltpu.SMEM)] * 2 + [vmem] * 6,
        out_specs=[vmem, vmem],
        out_shape=[
            jax.ShapeDtypeStruct((2, band, width), F32),
            jax.ShapeDtypeStruct((2, local, width), F32),
        ],
        scratch_shapes=[
            pltpu.VMEM((2, local, width), BF16),
            pltpu.VMEM((8, 128), jnp.int32),
            pltpu.VMEM((2, SG, local), F32),
            pltpu.VMEM((2, SG, local), F32),
            pltpu.VMEM((chips, 2, SG, width), F32),
            pltpu.VMEM((chips - 1, 2, SG, width), BF16),
            pltpu.VMEM((chips - 1, 2, SG, width), BF16),
            pltpu.VMEM((slabs, 2, band, width), F32),
            pltpu.VMEM((slabs, 2, band, width), BF16),
            pltpu.VMEM((slabs - 1, 2, band, width), BF16),
            pltpu.VMEM((3 * rows, width), F32),
            pltpu.VMEM((facets, slabs, 2, band, width), BF16),
            pltpu.VMEM((facets, 2, local, SG), BF16),
            dma((2,)), dma((2,)),
            dma((chips - 1,)), dma((chips - 1,)),
            dma((slabs - 1,)), dma((slabs - 1,)),
            dma((slabs - 1,)), dma((slabs - 1,)),
            dma((slabs, chips - 1)), dma((slabs, chips - 1)),
            dma((slabs, chips)), dma((slabs, chips)),
        ],
        compiler_params=pltpu.CompilerParams(collective_id=0, has_side_effects=True, vmem_limit_bytes=36 * 1024 * 1024),
        name="fused",
    )(subs, offset, subs[None, :], jnp.broadcast_to(offset, (8, 128)), slab, cells, values, weights)


def body(slab, facet_offset, subgrid_offset, vis_cell, vis_value, vis_weight):
    slabs = lax.axis_size("slab")
    facets = lax.axis_size("facet")
    local_rows = slab.shape[2]
    width = slab.shape[3]
    count_sub = subgrid_offset.shape[0]
    band = SG // slabs
    owned = count_sub * band // facets
    first = (facet_offset + lax.axis_index("slab") * local_rows).astype(jnp.int32)
    if owned == band and facets % 2 == 0 and facets > 2 and slabs > 1 and band % 16 == 0:
        residual, update = fused(
            facet_offset, subgrid_offset, slab[:, 0], vis_cell[0], vis_value[:, 0], vis_weight[0], slabs, facets
        )
        return (residual.reshape(2, 1, owned, width), update.reshape(2, 1, local_rows, width))
    sums = grid_visibilities(vis_cell[0], vis_value[:, 0, 0], vis_weight[0], owned, width)
    contrib = forward(first, subgrid_offset, slab[:, 0], slabs)
    contrib = contrib.reshape(2, slabs, facets, owned, width)
    parts = lax.all_to_all(contrib, "facet", 2, 2, tiled=True)
    parts = jnp.sum(parts, axis=2, dtype=F32).astype(BF16)
    parts = lax.all_to_all(parts, "slab", 1, 1, tiled=True)
    scale = 1.0 / math.sqrt(local_rows * slabs * facets)
    model = jnp.sum(parts, axis=1, dtype=F32) * scale
    residual = sums[:2] - sums[2:] * model
    sent = residual.astype(BF16).reshape(2, 1, 1, owned, width)
    piece = lax.all_gather(sent, "slab", axis=1, tiled=True)
    piece = lax.all_gather(piece, "facet", axis=2, tiled=True)
    piece = piece.reshape(2, slabs, count_sub, band, width)
    update = adjoint(first, subgrid_offset, piece, local_rows)
    return (residual.reshape(2, 1, owned, width), update.reshape(2, 1, local_rows, width))


def solution(mesh):
    placed = (
        P(None, "facet", "slab", None),
        P("facet"),
        P(),
        P("slab", "facet", None),
        P(None, "slab", "facet", None),
        P("slab", "facet", None),
    )
    return jax.shard_map(
        body,
        mesh=mesh,
        in_specs=placed,
        out_specs=(P(None, "slab", "facet", None), P(None, "facet", "slab", None)),
        check_vma=False,
    )
```

```python
import functools
import math

import jax
import jax.numpy as jnp
from jax import lax
from jax.experimental import pallas as pl
from jax.experimental.pallas import tpu as pltpu
from jax.sharding import PartitionSpec as P

IMAGE = 32768
SG = 256
UVSTEP = 16
F32 = jnp.float32
BF16 = jnp.bfloat16


def cis(turns):
    turns = turns & (IMAGE - 1)
    quarter = IMAGE // 4
    quad = (turns + quarter // 2) // quarter if quarter & (quarter - 1) else lax.shift_right_logical(
        turns + quarter // 2, quarter.bit_length() - 1
    )
    t = (turns - quad * quarter).astype(F32) * (2.0 * math.pi / IMAGE)
    z = t * t
    s = ((-1.9515295891e-4 * z + 8.3321608736e-3) * z - 1.6666654611e-1) * z * t + t
    c = ((2.443315711809948e-5 * z - 1.388731625493765e-3) * z + 4.166664568298827e-2) * z * z - 0.5 * z + 1.0
    odd = (quad & 1) == 1
    cos = jnp.where(odd, s, c)
    sin = jnp.where(odd, c, s)
    cos = jnp.where(((quad + 1) & 2) == 2, -cos, cos)
    sin = jnp.where((quad & 2) == 2, -sin, sin)
    return cos, sin


def grid_kernel(width, rows, cell_ref, value_ref, weight_ref, out_ref):
    @pl.when(pl.program_id(0) == 0)
    def _():
        out_ref[...] = jnp.zeros_like(out_ref)

    cell = cell_ref[...]
    weight = weight_ref[...]
    chunk = cell.shape[1]
    row = lax.shift_right_logical(cell, width.bit_length() - 1)
    col = cell & (width - 1)
    hot = jnp.where(lax.broadcasted_iota(jnp.int32, (width, chunk), 0) == col, 1.0, 0.0).astype(BF16)
    mine = lax.broadcasted_iota(jnp.int32, (rows, chunk), 0) == row
    terms = [weight * value_ref[0:1, :], weight * value_ref[1:2, :], weight]
    left = jnp.concatenate([jnp.where(mine, t, 0.0).astype(BF16) for t in terms], axis=0)
    out_ref[...] += lax.dot_general(left, hot, (((1,), (1,)), ((), ())), preferred_element_type=F32)


def grid_visibilities(cells, values, weights, owned, width):
    count = cells.shape[1]
    rows = -(-owned // 16) * 16
    chunk = min(count, 2048)
    out = pl.pallas_call(
        functools.partial(grid_kernel, width, rows),
        grid=(count // chunk,),
        in_specs=[
            pl.BlockSpec((1, chunk), lambda i: (0, i)),
            pl.BlockSpec((2, chunk), lambda i: (0, i)),
            pl.BlockSpec((1, chunk), lambda i: (0, i)),
        ],
        out_specs=pl.BlockSpec((3 * rows, width), lambda i: (0, 0)),
        out_shape=jax.ShapeDtypeStruct((3 * rows, width), F32),
        cost_estimate=pl.CostEstimate(flops=6 * rows * width * count, bytes_accessed=16 * count, transcendentals=0),
        name="gridding",
    )(cells, values, weights)
    return out.reshape(3, rows, width)[:, :owned]


def forward_kernel(first_ref, subs_ref, slab_ref, out_ref, cos_ref, sin_ref):
    s = pl.program_id(0)
    rows, local = cos_ref.shape
    first = first_ref[0]

    @pl.when(s == 0)
    def _():
        k = lax.broadcasted_iota(jnp.int32, (rows, local), 0)
        y = lax.broadcasted_iota(jnp.int32, (rows, local), 1) + first
        c, n = cis((UVSTEP * k) * y)
        cos_ref[...] = c
        sin_ref[...] = n

    y = lax.broadcasted_iota(jnp.int32, (8, local), 1) + first
    c1, s1 = cis(subs_ref[s] * y)
    c1, s1 = c1[0:1], s1[0:1]
    c2, s2 = cos_ref[...], sin_ref[...]
    tab_real = (c1 * c2 - s1 * s2).astype(BF16)
    tab_imag = (-(s1 * c2 + c1 * s2)).astype(BF16)
    re, im = slab_ref[0], slab_ref[1]
    dot = functools.partial(jnp.dot, preferred_element_type=F32)
    real = dot(tab_real, re) - dot(tab_imag, im)
    imag = dot(tab_real, im) + dot(tab_imag, re)
    slabs, band = out_ref.shape[1], out_ref.shape[3]
    for p in range(slabs):
        out_ref[0, p, 0] = real[p * band:(p + 1) * band].astype(out_ref.dtype)
        out_ref[1, p, 0] = imag[p * band:(p + 1) * band].astype(out_ref.dtype)


def forward(first, subs, slab, slabs):
    _, local, width = slab.shape
    count = subs.shape[0]
    band = SG // slabs
    return pl.pallas_call(
        forward_kernel,
        grid=(count,),
        in_specs=[
            pl.BlockSpec(memory_space=pltpu.SMEM),
            pl.BlockSpec(memory_space=pltpu.SMEM),
            pl.BlockSpec((2, local, width), lambda s: (0, 0, 0)),
        ],
        out_specs=pl.BlockSpec((2, slabs, 1, band, width), lambda s: (0, 0, s, 0, 0)),
        out_shape=jax.ShapeDtypeStruct((2, slabs, count, band, width), BF16),
        scratch_shapes=[pltpu.VMEM((SG, local), F32), pltpu.VMEM((SG, local), F32)],
        name="forward",
    )(first, subs, slab)


def adjoint_kernel(scale, slabs, first_ref, subs_ref, sent_ref, out_ref):
    tile = out_ref.shape[1]
    count = subs_ref.shape[1]
    band = SG // slabs
    start = first_ref[0] + pl.program_id(0) * tile
    yk = lax.broadcasted_iota(jnp.int32, (tile, SG), 0) + start
    c2, s2 = cis((UVSTEP * lax.broadcasted_iota(jnp.int32, (tile, SG), 1)) * yk)
    ys = lax.broadcasted_iota(jnp.int32, (tile, count), 0) + start
    c1, s1 = cis(ys * subs_ref[...])
    real = jnp.zeros(out_ref.shape[1:], F32)
    imag = jnp.zeros(out_ref.shape[1:], F32)
    dot = functools.partial(jnp.dot, preferred_element_type=F32)
    for s in range(count):
        a, b = c1[:, s:s + 1], s1[:, s:s + 1]
        tab_real = (a * c2 - b * s2).astype(BF16)
        tab_imag = (-(b * c2 + a * s2)).astype(BF16)
        re = jnp.concatenate([sent_ref[0, p, s] for p in range(slabs)], axis=0)
        im = jnp.concatenate([sent_ref[1, p, s] for p in range(slabs)], axis=0)
        real += dot(tab_real, re) + dot(tab_imag, im)
        imag += dot(tab_real, im) - dot(tab_imag, re)
    out_ref[0] = real * scale
    out_ref[1] = imag * scale


def adjoint(first, subs, sent, local):
    _, slabs, count, band, width = sent.shape
    tile = min(local, 256)
    return pl.pallas_call(
        functools.partial(adjoint_kernel, 1.0 / math.sqrt(count * SG), slabs),
        grid=(local // tile,),
        in_specs=[
            pl.BlockSpec(memory_space=pltpu.SMEM),
            pl.BlockSpec((1, count), lambda i: (0, 0)),
            pl.BlockSpec((2, slabs, count, band, width), lambda i: (0, 0, 0, 0, 0)),
        ],
        out_specs=pl.BlockSpec((2, tile, width), lambda i: (0, i, 0)),
        out_shape=jax.ShapeDtypeStruct((2, local, width), F32),
        name="adjoint",
    )(first, subs[None, :], sent)


def fused_kernel(
    scale, back, subs_ref, offset_ref, offv_ref, slab_hbm, cell_hbm, value_hbm, weight_hbm,
    residual_ref, update_ref,
    slab_ref, cell_ref, value_ref, weight_ref, in_sem, pslab, poff, cos_ref, sin_ref, acc, cb, rx, zf, zb, rz, sums, full, table,
    sw_send, sw_recv, x_send, x_recv, z_send, z_recv, gz_send, gz_recv, gx_send, gx_recv, gc_send, gc_recv,
):
    facets, slabs = lax.axis_size("facet"), lax.axis_size("slab")
    q, z = lax.axis_index("facet"), lax.axis_index("slab")
    core, chip = q % 2, q // 2
    chips = facets // 2
    partner = q + 1 - 2 * core
    loads = [
        pltpu.make_async_copy(src, dst, in_sem.at[n])
        for n, (src, dst) in enumerate([
            (slab_hbm, slab_ref), (cell_hbm, cell_ref), (value_hbm, value_ref), (weight_hbm, weight_ref),
        ])
    ]
    for load in loads:
        load.start()
    _, local, width = slab_ref.shape
    band = SG // slabs
    dot = functools.partial(jnp.dot, preferred_element_type=F32)

    def at_chip(d):
        return 2 * ((chip + d) % chips) + core

    def from_chip(d):
        return 2 * ((chip + chips - d) % chips) + core

    def at_slab(e):
        return (z + e) % slabs

    def from_slab(e):
        return (z + slabs - e) % slabs

    def remote(src, dst, send, recv, **where):
        return pltpu.make_async_remote_copy(
            src_ref=src, dst_ref=dst, send_sem=send, recv_sem=recv,
            device_id=where, device_id_type=pl.DeviceIdType.MESH,
        )

    barrier = pltpu.get_barrier_semaphore()
    pl.semaphore_signal(barrier, inc=1, device_id={"facet": partner}, device_id_type=pl.DeviceIdType.MESH)
    for d in range(1, chips):
        pl.semaphore_signal(barrier, inc=1, device_id={"facet": at_chip(d)}, device_id_type=pl.DeviceIdType.MESH)
    for e in range(1, slabs):
        pl.semaphore_signal(barrier, inc=1, device_id={"slab": at_slab(e)}, device_id_type=pl.DeviceIdType.MESH)
    pl.semaphore_wait(barrier, chips + slabs - 1)

    swap_offset = remote(offv_ref, poff, sw_send.at[0], sw_recv.at[0], facet=partner)
    swap_slab = remote(slab_hbm, pslab, sw_send.at[1], sw_recv.at[1], facet=partner)
    swap_offset.start()
    swap_slab.start()

    first = offset_ref[0] + z * local

    def build(y, slot):
        def step(i, carry):
            k = lax.broadcasted_iota(jnp.int32, (32, local), 0) + i * 32
            c, n = cis((UVSTEP * k) * y[0:1, :])
            at = pl.ds(pl.multiple_of(i * 32, 32), 32)
            cos_ref[slot, at] = c
            sin_ref[slot, at] = n
            return carry

        lax.fori_loop(0, SG // 32, step, 0)

    def partial_sum(s, y, slot, data_ref):
        c1, s1 = cis(subs_ref[s] * y)
        c1, s1 = c1[0:1], s1[0:1]
        c2, s2 = cos_ref[slot], sin_ref[slot]
        tab_real = (c1 * c2 - s1 * s2).astype(BF16)
        tab_imag = (-(s1 * c2 + c1 * s2)).astype(BF16)
        re, im = data_ref[0], data_ref[1]
        return dot(tab_real, re) - dot(tab_imag, im), dot(tab_real, im) + dot(tab_imag, re)

    line = lax.broadcasted_iota(jnp.int32, (8, local), 1)
    places = line + first
    build(places, 0)

    def own_part(d, carry):
        real, imag = partial_sum(at_chip(d), places, 0, slab_ref)
        acc[d, 0] = real
        acc[d, 1] = imag
        return carry

    loads[0].wait()
    lax.fori_loop(0, chips, own_part, 0)
    swap_offset.wait()
    pplaces = line + (poff[:, 0:1] + z * local)
    build(pplaces, 1)
    swap_slab.wait()
    x_copies = []
    for d in list(range(1, chips)) + [0]:
        real, imag = partial_sum(at_chip(d), pplaces, 1, pslab)
        if d == 0:
            acc[0, 0] += real
            acc[0, 1] += imag
        else:
            cb[d - 1, 0] = (acc[d, 0] + real).astype(BF16)
            cb[d - 1, 1] = (acc[d, 1] + imag).astype(BF16)
            copy = remote(cb.at[d - 1], rx.at[d - 1], x_send.at[d - 1], x_recv.at[d - 1], facet=at_chip(d))
            copy.start()
            x_copies.append(copy)

    rows = sums.shape[0] // 3
    count = cell_ref.shape[1]
    chunk = min(count, 2048)
    sums[...] = jnp.zeros_like(sums)

    def grid_step(i, carry):
        at = pl.ds(pl.multiple_of(i * chunk, chunk), chunk)
        cell = cell_ref[:, at]
        weight = weight_ref[:, at]
        row = lax.shift_right_logical(cell, width.bit_length() - 1).astype(F32)
        col = (cell & (width - 1)).astype(F32)
        lines = lax.broadcasted_iota(jnp.int32, (16, chunk), 0).astype(F32).astype(BF16)
        row = jnp.broadcast_to(row, (16, chunk)).astype(BF16)
        col = jnp.broadcast_to(col, (16, chunk)).astype(BF16)
        one, zero = jnp.ones((16, chunk), BF16), jnp.zeros((16, chunk), BF16)
        hot = jnp.concatenate(
            [jnp.where(col == lines + jnp.asarray(g, BF16), one, zero) for g in range(0, width, 16)], axis=0
        )
        terms = [weight * value_ref[0, :, at], weight * value_ref[1, :, at], weight]
        terms = [jnp.broadcast_to(t, (16, chunk)).astype(BF16) for t in terms]
        left = jnp.concatenate(
            [jnp.where(row == lines + jnp.asarray(g, BF16), t, zero) for t in terms for g in range(0, rows, 16)],
            axis=0,
        )
        sums[...] += lax.dot_general(left, hot, (((1,), (1,)), ((), ())), preferred_element_type=F32)
        return carry

    for load in loads[1:]:
        load.wait()
    chunks = count // chunk
    early = (5 * chunks) // 8
    lax.fori_loop(0, early, grid_step, 0)

    for copy in x_copies:
        copy.wait()
    for p in range(slabs):
        for c in range(2):
            at = slice(p * band, (p + 1) * band)
            total = acc[0, c, at]
            for d in range(1, chips):
                total += rx[d - 1, c, at].astype(F32)
            zf[p, c] = total
            zb[p, c] = total.astype(BF16)
    z_copies = []
    for e in range(1, slabs):
        copy = remote(zb.at[at_slab(e)], rz.at[e - 1], z_send.at[e - 1], z_recv.at[e - 1], slab=at_slab(e))
        copy.start()
        z_copies.append(copy)

    tile = min(local, 256)

    lax.fori_loop(early, chunks, grid_step, 0)

    for copy in z_copies:
        copy.wait()
    for c in range(2):
        model = zf[z, c]
        for e in range(1, slabs):
            model += rz[e - 1, c].astype(F32)
        piece = sums[c * rows:c * rows + band] - sums[2 * rows:2 * rows + band] * (model * scale)
        residual_ref[c] = piece
        full[q, z, c] = piece.astype(BF16)

    def table_step(i, carry):
        at = pl.ds(pl.multiple_of(i * tile, tile), tile)
        y = lax.broadcasted_iota(jnp.int32, (tile, 1), 0) + (first + i * tile)
        c2, s2 = cis((UVSTEP * lax.broadcasted_iota(jnp.int32, (tile, SG), 1)) * y)
        lane = lax.broadcasted_iota(jnp.int32, (1, facets), 1)
        subs = jnp.zeros((1, facets), jnp.int32)
        for s in range(facets):
            subs = jnp.where(lane == s, subs_ref[s], subs)
        c1, s1 = cis(y * subs)
        for s in range(facets):
            a, b = c1[:, s:s + 1], s1[:, s:s + 1]
            table[s, 0, at] = (a * c2 - b * s2).astype(BF16)
            table[s, 1, at] = (-(b * c2 + a * s2)).astype(BF16)
        return carry

    late = []

    def spread(s, p, e, d):
        ref = full.at[s, p]
        copy = remote(ref, ref, gc_send.at[e, d], gc_recv.at[e, d], facet=partner)
        copy.start()
        late.append(copy)

    def across(p, e):
        ref = full.at[q, p]
        out = []
        for d in range(1, chips):
            copy = remote(ref, ref, gx_send.at[e, d - 1], gx_recv.at[e, d - 1], facet=at_chip(d))
            copy.start()
            out.append(copy)
        return out

    own = full.at[q, z]
    g_copies = []
    for e in range(1, slabs):
        copy = remote(own, own, gz_send.at[e - 1], gz_recv.at[e - 1], slab=at_slab(e))
        copy.start()
        g_copies.append(copy)
    a_copies = [across(z, 0)]
    spread(q, z, 0, 0)
    tiles = local // tile
    done = 0
    for e in range(1, slabs):
        share = (e * tiles) // slabs
        lax.fori_loop(done, share, table_step, 0)
        done = share
        g_copies[e - 1].wait_recv()
        a_copies.append(across(from_slab(e), e))
        spread(q, from_slab(e), e, 0)
    lax.fori_loop(done, tiles, table_step, 0)

    def update_pass(which, begin, end):
        def step(i, carry):
            at = pl.ds(pl.multiple_of(i * tile, tile), tile)
            real = imag = None
            for s in which:
                tab_real, tab_imag = table[s, 0, at], table[s, 1, at]
                re = jnp.concatenate([full[s, p, 0] for p in range(slabs)], axis=0)
                im = jnp.concatenate([full[s, p, 1] for p in range(slabs)], axis=0)
                dr = dot(tab_real, re) + dot(tab_imag, im)
                di = dot(tab_real, im) - dot(tab_imag, re)
                real = dr if real is None else real + dr
                imag = di if imag is None else imag + di
            if not begin:
                real += update_ref[0, at]
                imag += update_ref[1, at]
            update_ref[0, at] = real * back if end else real
            update_ref[1, at] = imag * back if end else imag
            return carry

        lax.fori_loop(0, tiles, step, 0)

    def relay(e):
        for d in range(1, chips):
            a_copies[e][d - 1].wait_recv()
            spread(from_chip(d), from_slab(e), e, d)

    relay(0)
    update_pass([q], True, False)
    for e in range(1, slabs - 1):
        relay(e)
    for copy in late[:slabs]:
        copy.wait_recv()
    update_pass([partner], False, False)
    relay(slabs - 1)
    update_pass([from_chip(d) for d in range(1, chips)], False, False)
    for copy in late[slabs:]:
        copy.wait_recv()
    update_pass([from_chip(d) + 1 - 2 * core for d in range(1, chips)], False, True)
    for copy in g_copies + late:
        copy.wait_send()
    for group in a_copies:
        for copy in group:
            copy.wait_send()


def fused(offset, subs, slab, cells, values, weights, slabs, facets):
    _, local, width = slab.shape
    band = SG // slabs
    chips = facets // 2
    rows = -(-band // 16) * 16
    vmem = pl.BlockSpec(memory_space=pltpu.VMEM)
    dma = pltpu.SemaphoreType.DMA
    return pl.pallas_call(
        functools.partial(
            fused_kernel, 1.0 / math.sqrt(local * slabs * facets), 1.0 / math.sqrt(subs.shape[0] * SG)
        ),
        in_specs=[pl.BlockSpec(memory_space=pltpu.SMEM)] * 2 + [vmem] + [pl.BlockSpec(memory_space=pltpu.HBM)] * 4,
        out_specs=[vmem, vmem],
        out_shape=[
            jax.ShapeDtypeStruct((2, band, width), F32),
            jax.ShapeDtypeStruct((2, local, width), F32),
        ],
        scratch_shapes=[
            pltpu.VMEM(slab.shape, slab.dtype),
            pltpu.VMEM(cells.shape, cells.dtype),
            pltpu.VMEM(values.shape, values.dtype),
            pltpu.VMEM(weights.shape, weights.dtype),
            dma((4,)),
            pltpu.VMEM((2, local, width), BF16),
            pltpu.VMEM((8, 128), jnp.int32),
            pltpu.VMEM((2, SG, local), F32),
            pltpu.VMEM((2, SG, local), F32),
            pltpu.VMEM((chips, 2, SG, width), F32),
            pltpu.VMEM((chips - 1, 2, SG, width), BF16),
            pltpu.VMEM((chips - 1, 2, SG, width), BF16),
            pltpu.VMEM((slabs, 2, band, width), F32),
            pltpu.VMEM((slabs, 2, band, width), BF16),
            pltpu.VMEM((slabs - 1, 2, band, width), BF16),
            pltpu.VMEM((3 * rows, width), F32),
            pltpu.VMEM((facets, slabs, 2, band, width), BF16),
            pltpu.VMEM((facets, 2, local, SG), BF16),
            dma((2,)), dma((2,)),
            dma((chips - 1,)), dma((chips - 1,)),
            dma((slabs - 1,)), dma((slabs - 1,)),
            dma((slabs - 1,)), dma((slabs - 1,)),
            dma((slabs, chips - 1)), dma((slabs, chips - 1)),
            dma((slabs, chips)), dma((slabs, chips)),
        ],
        compiler_params=pltpu.CompilerParams(collective_id=0, has_side_effects=True, vmem_limit_bytes=60 * 1024 * 1024),
        name="fused",
    )(subs, offset, jnp.broadcast_to(offset, (8, 128)), slab, cells, values, weights)


def body(slab, facet_offset, subgrid_offset, vis_cell, vis_value, vis_weight):
    slabs = lax.axis_size("slab")
    facets = lax.axis_size("facet")
    local_rows = slab.shape[2]
    width = slab.shape[3]
    count_sub = subgrid_offset.shape[0]
    band = SG // slabs
    owned = count_sub * band // facets
    first = (facet_offset + lax.axis_index("slab") * local_rows).astype(jnp.int32)
    if owned == band and facets % 2 == 0 and facets > 2 and slabs > 1 and band % 16 == 0:
        residual, update = fused(
            facet_offset, subgrid_offset, slab[:, 0], vis_cell[0], vis_value[:, 0], vis_weight[0], slabs, facets
        )
        return (residual.reshape(2, 1, owned, width), update.reshape(2, 1, local_rows, width))
    sums = grid_visibilities(vis_cell[0], vis_value[:, 0, 0], vis_weight[0], owned, width)
    contrib = forward(first, subgrid_offset, slab[:, 0], slabs)
    contrib = contrib.reshape(2, slabs, facets, owned, width)
    parts = lax.all_to_all(contrib, "facet", 2, 2, tiled=True)
    parts = jnp.sum(parts, axis=2, dtype=F32).astype(BF16)
    parts = lax.all_to_all(parts, "slab", 1, 1, tiled=True)
    scale = 1.0 / math.sqrt(local_rows * slabs * facets)
    model = jnp.sum(parts, axis=1, dtype=F32) * scale
    residual = sums[:2] - sums[2:] * model
    sent = residual.astype(BF16).reshape(2, 1, 1, owned, width)
    piece = lax.all_gather(sent, "slab", axis=1, tiled=True)
    piece = lax.all_gather(piece, "facet", axis=2, tiled=True)
    piece = piece.reshape(2, slabs, count_sub, band, width)
    update = adjoint(first, subgrid_offset, piece, local_rows)
    return (residual.reshape(2, 1, owned, width), update.reshape(2, 1, local_rows, width))


def solution(mesh):
    placed = (
        P(None, "facet", "slab", None),
        P("facet"),
        P(),
        P("slab", "facet", None),
        P(None, "slab", "facet", None),
        P("slab", "facet", None),
    )
    return jax.shard_map(
        body,
        mesh=mesh,
        in_specs=placed,
        out_specs=(P(None, "slab", "facet", None), P(None, "facet", "slab", None)),
        check_vma=False,
    )
```
